32 devices in a mesh: groups: 2 (over y), tm: 4 (over z), batch: 2 (over x), rep: 2 (over core).
Axes of the slice: x: 2, y: 2, z: 4, core: 2. Of those that a mesh axis runs over, the one named last changes fastest.
Arguments:
- latents: bfloat16 [8, 2048, 512], P(('groups', 'batch', 'rep'), 'tm'), parts along dimension 0, may hold values from -6 to 6
- session_ids: int32 [8], P(('groups', 'batch', 'rep')), parts along dimension 0, may hold values from 0 to 7
- session_gain: float32 [8, 512], replicated, may hold values from 0.25 to 1.75
- session_shift: float32 [8, 512], replicated, may hold values from -3 to 3
- first_conv_weight: bfloat16 [3, 512, 512], replicated, may hold values from -0.15625 to 0.15625
- first_conv_bias: float32 [512], replicated, may hold values from -1.5 to 1.5
- second_conv_weight: bfloat16 [3, 512, 512], replicated, may hold values from -0.15625 to 0.15625
- second_conv_bias: float32 [512], replicated, may hold values from -1.5 to 1.5
- proj_weight: bfloat16 [512, 128], replicated, may hold values from -0.25 to 0.25
- offsets: int32 [8, 2048], P(('groups', 'batch', 'rep'), 'tm'), parts along dimension 0, may hold values from 1 to 10
- counts: int32 [8, 4], P(('groups', 'batch', 'rep'), 'tm'), parts along dimension 0, may hold values from 128 to 512, as said below
Outputs:
- embedding: bfloat16 [8, 2048, 128], P(('groups', 'batch', 'rep'), 'tm'), parts along dimension 0
- grad_conv: float32 [6, 512, 512], P('groups', None, 'tm'), parts along dimension 0
- grad_bias: float32 [1024], P(('groups', 'tm')), parts along dimension 0
- grad_proj: float32 [1024, 128], P(('groups', 'tm')), parts along dimension 0
The draws below stay inside these ranges and needn't reach their ends.
There are 2 independent parts, one for each index of `groups`. The reference program is written for one: setup_inputs(seed, part) draws one part's arguments, and reference() takes and returns one part's arrays. A program takes and returns all parts, laid end to end along the dimension named above; an argument that names none is the same for every part. Nothing has to cross between parts.
Inputs may be any that keep to these rules, and one draw needn't show every extreme that they name: `counts`: bin t of a slab is live when t is below the slab's count.
All inputs are finite; a program needn't handle non-finite values.
Results may differ from the reference program's by a relative error of at most 0.0063.
Values may be sent and summed in bfloat16 or wider, within the bound.
A program may use at most 64 MiB of HBM per device.

```python
import jax
import jax.numpy as jnp
from jax import lax

C = 512
EMB = 128
SESS = 8
TBIN = 512
FIRST_DILATION = 1
SECOND_DILATION = 2
OFF_MAX = 10
W = 4
SLABS = 4
WINDOW_BINS = 2048
N_BATCH = 2
N_REP = 2


def draw_session_ids(key, part):
    labels = jax.random.randint(key, (W,), 0, SESS)
    return labels.at[0].set(0).at[W - 1].set(SESS - 1)


def draw_offsets(key, part):
    values = jax.random.randint(key, (W, WINDOW_BINS), 1, OFF_MAX + 1)
    return values.at[0, 0].set(OFF_MAX).at[0, 1].set(1)


def draw_counts(key, part):
    values = jax.random.randint(key, (W, SLABS), TBIN // 4, TBIN + 1)
    return values.at[0, 0].set(TBIN).at[W - 1, SLABS - 1].set(TBIN // 4)


def block_scale(stream_key, dims, pieces, least, high):
    loudness = 1.0
    for position, blocks in pieces:
        draws = jax.random.uniform(jax.random.fold_in(jax.random.fold_in(stream_key, 6), position), (blocks,), jnp.float32, least / len(pieces), high / len(pieces))
        loudness = loudness * jnp.repeat(jnp.exp(draws), dims[position] // blocks).reshape((-1,) + (1,) * (len(dims) - 1 - position))
    return loudness


def scatter_about(key, dims, spread, limit, pieces=(), dtype=jnp.bfloat16):
    factor_of = block_scale(key, dims, pieces, -0.22, 0.18) if pieces else 1.0
    entries = jax.random.normal(key, dims, jnp.float32) * spread * factor_of
    return jnp.minimum(jnp.maximum(entries, -limit), limit).astype(dtype)


def setup_inputs(seed: int = 0, part: int = 0) -> dict:
    keys = jax.random.split(jax.random.key(seed), 12)
    part_keys = jax.random.split(jax.random.fold_in(keys[11], part), 12)
    return {
        "latents": scatter_about(part_keys[0], (W, WINDOW_BINS, C), 1.0, 6.0, ((0, 4), (1, 4))),
        "session_ids": draw_session_ids(jax.random.fold_in(jax.random.fold_in(keys[11], part), 71), part),
        "session_gain": jnp.clip(1.0 + 0.15 * jax.random.normal(keys[2], (SESS, C), jnp.float32), 0.25, 1.75),
        "session_shift": scatter_about(keys[3], (SESS, C), 0.5, 3.0, (), jnp.float32),
        "first_conv_weight": scatter_about(keys[4], (3, C, C), (3 * C) ** -0.5, 0.15625),
        "first_conv_bias": scatter_about(keys[5], (C,), 0.3, 1.5, (), jnp.float32),
        "second_conv_weight": scatter_about(keys[6], (3, C, C), (3 * C) ** -0.5, 0.15625),
        "second_conv_bias": scatter_about(keys[7], (C,), 0.3, 1.5, (), jnp.float32),
        "proj_weight": scatter_about(keys[8], (C, EMB), C ** -0.5, 0.25),
        "offsets": draw_offsets(jax.random.fold_in(jax.random.fold_in(keys[11], part), 71), part),
        "counts": draw_counts(jax.random.fold_in(jax.random.fold_in(keys[11], part), 71), part),
    }


reciprocal_softness = 2.0

def convolved_rows(padded, couple_coefficient, bias, dilation, count):
    total = jnp.zeros((count, couple_coefficient.shape[2]), jnp.float32) + bias[None, :]
    for filter_tap_index in range(3):
        shifted = padded[filter_tap_index * dilation:filter_tap_index * dilation + count]
        total = total + jnp.dot(shifted, couple_coefficient[filter_tap_index], preferred_element_type=jnp.float32)
    return total

def pool_pass(item):
    aggregated_latent_code, aggregated_usable_mask = item
    cosine_affinity_matrix = reciprocal_softness * jnp.dot(aggregated_latent_code, aggregated_latent_code.T, preferred_element_type=jnp.float32)
    count = aggregated_latent_code.shape[0]
    counterpart_latent_code = jnp.arange(count)[:, None] != jnp.arange(count)[None, :]
    couple_coefficient = jnp.where(counterpart_latent_code, jnp.exp(cosine_affinity_matrix - reciprocal_softness), 0.0) * aggregated_usable_mask[None, :]
    denom = lax.optimization_barrier(jnp.sum(couple_coefficient, axis=1))
    soft = (couple_coefficient / denom[:, None]).astype(jnp.bfloat16)
    query_sample_vector = jnp.dot(soft, aggregated_latent_code, preferred_element_type=jnp.float32)
    reverse = (couple_coefficient * aggregated_usable_mask[:, None] / denom[None, :]).astype(jnp.bfloat16)
    aggregated_result = jnp.dot(reverse, aggregated_latent_code, preferred_element_type=jnp.float32)
    return (query_sample_vector, aggregated_result)

def to_pools(values):
    trailing = values.shape[2:]
    grid = values.reshape((N_BATCH, N_REP, SLABS, TBIN) + trailing)
    grid = jnp.moveaxis(grid, 0, 2)
    return grid.reshape((N_REP * SLABS, N_BATCH * TBIN) + trailing)

def from_pools(values):
    trailing = values.shape[2:]
    grid = values.reshape((N_REP, SLABS, N_BATCH, TBIN) + trailing)
    grid = jnp.moveaxis(grid, 2, 0)
    return grid.reshape((W, WINDOW_BINS) + trailing)

def reference(latents, session_ids, session_gain, session_shift, first_conv_weight, first_conv_bias, second_conv_weight, second_conv_bias, proj_weight, offsets, counts):
    gains = session_gain[session_ids][:, None, :]
    shifts = session_shift[session_ids][:, None, :]
    base_offset = (latents.astype(jnp.float32) * gains + shifts).astype(jnp.bfloat16)

    def window_pass(starting_rows):
        input_padded = jnp.pad(starting_rows, ((FIRST_DILATION, FIRST_DILATION), (0, 0)))
        first_preactivation = convolved_rows(input_padded, first_conv_weight, first_conv_bias, FIRST_DILATION, WINDOW_BINS)
        first_hidden = (starting_rows.astype(jnp.float32) + jax.nn.gelu(first_preactivation)).astype(jnp.bfloat16)
        first_padded = jnp.pad(first_hidden, ((SECOND_DILATION, SECOND_DILATION), (0, 0)))
        second_preactivation = convolved_rows(first_padded, second_conv_weight, second_conv_bias, SECOND_DILATION, WINDOW_BINS)
        hidden_two = (first_hidden.astype(jnp.float32) + jax.nn.gelu(second_preactivation)).astype(jnp.bfloat16)
        feats = jnp.dot(hidden_two, proj_weight, preferred_element_type=jnp.float32)
        scale = lax.rsqrt(lax.optimization_barrier(jnp.sum(feats * feats, axis=1)) + 1e-06)
        unit = feats * scale[:, None]
        return (first_padded, second_preactivation, hidden_two, unit, scale)
    first_padded, second_preactivation, hidden_two, unit, scale = lax.map(window_pass, base_offset)
    embed = unit.astype(jnp.bfloat16)
    moment = jnp.arange(WINDOW_BINS)
    usable_mask_vector = ((moment % TBIN)[None, :] < jnp.repeat(counts, TBIN, axis=1)).astype(jnp.float32)
    back_time = moment[None, :] - offsets
    target = jnp.where(back_time >= 0, back_time, moment[None, :] + offsets)
    matched_sample_vector = jnp.take_along_axis(embed, target[:, :, None], axis=1).astype(jnp.float32)
    query_sample_vector, aggregated_result = lax.map(pool_pass, (to_pools(embed), to_pools(usable_mask_vector)))
    query_sample_vector = from_pools(query_sample_vector)
    aggregated_result = from_pools(aggregated_result)

    def push_window(target_row, values):
        return jnp.zeros((WINDOW_BINS, EMB), jnp.float32).at[target_row].add(values)
    propagated_samples = jax.vmap(push_window)(target, usable_mask_vector[:, :, None] * embed.astype(jnp.float32))
    unit_length_derivative = reciprocal_softness * (usable_mask_vector[:, :, None] * (query_sample_vector - matched_sample_vector) + aggregated_result - propagated_samples)
    along = lax.optimization_barrier(jnp.sum(unit * unit_length_derivative, axis=2, keepdims=True))
    grad_feat = ((unit_length_derivative - unit * along) * scale[:, :, None]).astype(jnp.bfloat16)
    grad_proj = jnp.dot(hidden_two.reshape(-1, C).T, grad_feat.reshape(-1, EMB), preferred_element_type=jnp.float32)

    def window_back(carry, item):
        rows_with_padding, pre_rows, feat_rows = item
        grad_hidden = jnp.dot(feat_rows, proj_weight.T, preferred_element_type=jnp.float32)
        unused, pull = jax.vjp(jax.nn.gelu, pre_rows)
        gradient_preactivation = pull(grad_hidden)[0].astype(jnp.bfloat16)
        conv_sum, bias_sum = carry
        filter_taps = jnp.stack([jnp.dot(rows_with_padding[filter_tap_index * SECOND_DILATION:filter_tap_index * SECOND_DILATION + WINDOW_BINS].T, gradient_preactivation, preferred_element_type=jnp.float32) for filter_tap_index in range(3)])
        return ((conv_sum + filter_taps, bias_sum + lax.optimization_barrier(jnp.sum(gradient_preactivation.astype(jnp.float32), axis=0))), None)
    start_carry = (jnp.zeros((3, C, C), jnp.float32), jnp.zeros((C,), jnp.float32))
    (grad_conv, grad_bias), unused_out = lax.scan(window_back, start_carry, (first_padded, second_preactivation, grad_feat))
    return (embed, grad_conv, grad_bias, grad_proj)
```

```python
import functools
import types

import jax
import jax.numpy as jnp
from jax import lax
from jax.experimental import pallas as pl
from jax.experimental.pallas import tpu as pltpu
from jax.sharding import PartitionSpec as P

HALO = 16
PAD = 8
LANES = 128
F32 = jnp.float32
BF16 = jnp.bfloat16
GELU_C = 0.7978845608028654
GELU_A = 0.044715
HALVES = 2
INNER_BLOCKS = 2
TM_FIRST = 0


def gelu_parts(x):
    square = x * x
    th = jnp.tanh(GELU_C * x * (1.0 + GELU_A * square))
    half = 0.5 * (1.0 + th)
    slope = half + (0.5 * GELU_C) * x * (1.0 - th * th) * (1.0 + (3.0 * GELU_A) * square)
    return x * half, slope


def kernel(n_tm, n_batch, names, *refs):
    s = types.SimpleNamespace(**dict(zip(names, refs, strict=True)))
    rows, channels = s.lat.shape
    total = rows + 2 * HALO
    share = channels // n_tm
    span = channels // HALVES
    half = span // 2
    piece = half // n_batch
    chunks = 3 * HALVES
    extra = s.p_grads.shape[2]
    body = extra - HALO
    z = lax.axis_index("tm")
    b = lax.axis_index("batch")
    r = lax.axis_index("rep")
    other = 1 - r

    def tm_at(o):
        return {"tm": lax.rem(z + o, n_tm)}

    def batch_at(o):
        return {"batch": lax.rem(b + o, n_batch)}

    def across_at(o):
        return {"batch": lax.rem(b + o, n_batch), "rep": other}

    barrier = pltpu.get_barrier_semaphore()
    peers = [tm_at(o) for o in range(1, n_tm)] + [{"rep": other}]
    peers += [batch_at(o) for o in range(1, n_batch)] + [across_at(o) for o in range(1, n_batch)]
    for peer in peers:
        pl.semaphore_signal(barrier, inc=1, device_id=peer, device_id_type=pl.DeviceIdType.MESH)

    loads = {}
    for i, name in enumerate(("lat", "gain", "shift", "sid", "cnt", "off", "b1", "w1", "w2", "b2", "proj")):
        loads[name] = pltpu.make_async_copy(getattr(s, name + "_hbm"), getattr(s, name), s.load_sem.at[i])
        loads[name].start()

    pl.semaphore_wait(barrier, len(peers))
    started = []

    def send(src, dst, sems, index, peer):
        copy = pltpu.make_async_remote_copy(
            src_ref=src, dst_ref=dst, send_sem=sems.at[(0,) + index], recv_sem=sems.at[(1,) + index],
            device_id=peer, device_id_type=pl.DeviceIdType.MESH,
        )
        copy.start()
        started.append(copy)
        return copy

    low = send(s.lat_hbm.at[pl.ds(rows - HALO, HALO)], s.halo.at[0], s.halo_sem, (0,), tm_at(1))
    high = send(s.lat_hbm.at[pl.ds(0, HALO)], s.halo.at[1], s.halo_sem, (1,), tm_at(n_tm - 1))

    s.ext[0:PAD, :] = jnp.zeros((PAD, channels), F32)
    s.ext[PAD + total :, :] = jnp.zeros((PAD, channels), F32)
    s.hid[0:PAD, :] = jnp.zeros((PAD, channels), F32)
    s.hid[PAD + total :, :] = jnp.zeros((PAD, channels), F32)
    has_low = z > 0
    has_high = z < n_tm - 1

    for name in ("gain", "shift", "sid", "cnt", "off"):
        loads[name].wait()
    own_count = s.cnt[0, 0]
    s.meta[0:1, :] = s.off[0:1, 0:LANES]
    s.meta[1:2, :] = jnp.full((1, LANES), own_count, jnp.int32)
    s.meta[2:8, :] = jnp.zeros((6, LANES), jnp.int32)
    nextm = send(s.meta, s.meta_next, s.meta_sem, (0,), tm_at(n_tm - 1))
    mpools = [send(s.meta, s.meta_pool.at[o - 1], s.mpool_sem, (o - 1,), batch_at(o)) for o in range(1, n_batch)]
    pick = lax.broadcasted_iota(jnp.int32, s.gain.shape, 0) == s.sid[0]
    gain = jnp.sum(jnp.where(pick, s.gain[...], 0.0), axis=0, keepdims=True)
    shift = jnp.sum(jnp.where(pick, s.shift[...], 0.0), axis=0, keepdims=True)

    def based(block):
        return (block.astype(F32) * gain + shift).astype(BF16).astype(F32)

    def gather_taps(source, dilation, begin, count):
        for k in range(3):
            first = PAD + begin + (k - 1) * dilation
            s.taps[begin : begin + count, k * channels : (k + 1) * channels] = source[first : first + count, :].astype(
                BF16
            )

    def first_hidden(begin, count):
        x = s.pre[begin : begin + count, :] + s.b1[...]
        value = 0.5 * x * (1.0 + jnp.tanh(GELU_C * x * (1.0 + GELU_A * x * x)))
        return (s.ext[PAD + begin : PAD + begin + count, :] + value).astype(BF16).astype(F32)

    def second_hidden(begin, count):
        value, deriv = gelu_parts(s.pre[begin : begin + count, :] + s.b2[...])
        s.slope[begin : begin + count, :] = deriv
        hid = (s.hid[PAD + begin : PAD + begin + count, :] + value).astype(BF16)
        s.hid2[begin : begin + count, :] = hid
        feats = jnp.dot(hid, s.proj[...], preferred_element_type=F32)
        scale = lax.rsqrt(jnp.sum(feats * feats, axis=1, keepdims=True) + 1e-06)
        unit = feats * scale
        s.unit[begin : begin + count, :] = unit
        s.scale[begin : begin + count, :] = jnp.broadcast_to(scale, (count, LANES))
        s.emb_ext[begin : begin + count, :] = unit.astype(BF16)

    pools = []

    def send_pool(first, count):
        at = pl.ds(first, count)
        i = len(pools)
        s.pool[0, first : first + count, :] = s.emb_ext[HALO + first : HALO + first + count, :]
        pools.append([
            send(s.pool.at[0, at], s.pool.at[o, at], s.pool_sem, (i, o - 1), batch_at(o)) for o in range(1, n_batch)
        ])

    loads["lat"].wait()
    s.ext[PAD + HALO : PAD + HALO + rows, :] = based(s.lat[...])
    near, near_rows = HALO + PAD, rows - 2 * PAD
    gather_taps(s.ext, 1, near, near_rows)
    loads["b1"].wait()
    loads["w1"].wait()
    s.pre[near : near + near_rows, :] = jnp.dot(
        s.taps[near : near + near_rows, :], s.w1[...], preferred_element_type=F32
    )
    s.hid[PAD + near : PAD + near + near_rows, :] = first_hidden(near, near_rows)
    block = (rows - 2 * HALO) // INNER_BLOCKS
    for name in ("w2", "b2", "proj"):
        loads[name].wait()
    for i in range(INNER_BLOCKS):
        begin = 2 * HALO + i * block
        gather_taps(s.hid, 2, begin, block)
        s.pre[begin : begin + block, :] = jnp.dot(
            s.taps[begin : begin + block, :], s.w2[...], preferred_element_type=F32
        )
        second_hidden(begin, block)
        send_pool(begin - HALO, block)

    edge_rows = 2 * HALO
    last = total - edge_rows
    low.wait_recv()
    high.wait_recv()
    s.ext[PAD : PAD + HALO, :] = jnp.where(has_low, based(s.halo[0]), 0.0)
    s.ext[PAD + HALO + rows : PAD + total, :] = jnp.where(has_high, based(s.halo[1]), 0.0)

    def conv_ends(source, dilation, weight):
        gather_taps(source, dilation, 0, edge_rows)
        gather_taps(source, dilation, last, edge_rows)
        ends = jnp.concatenate([s.taps[0:edge_rows, :], s.taps[last:, :]], axis=0)
        ends = jnp.dot(ends, weight[...], preferred_element_type=F32)
        s.pre[0:edge_rows, :] = ends[0:edge_rows, :]
        s.pre[last:, :] = ends[edge_rows:, :]

    conv_ends(s.ext, 1, s.w1)
    at = lax.broadcasted_iota(jnp.int32, (edge_rows, 1), 0)
    s.hid[PAD : PAD + edge_rows, :] = jnp.where(
        jnp.logical_or(has_low, at >= HALO), first_hidden(0, edge_rows), 0.0
    )
    s.hid[PAD + last : PAD + total, :] = jnp.where(
        jnp.logical_or(has_high, at < HALO), first_hidden(last, edge_rows), 0.0
    )
    conv_ends(s.hid, 2, s.w2)
    second_hidden(0, edge_rows)
    second_hidden(last, edge_rows)
    send_pool(0, HALO)
    send_pool(rows - HALO, HALO)
    own = s.pool[0]
    store = pltpu.make_async_copy(s.pool.at[0], s.emb_out, s.store_sem)
    store.start()

    for k in range(3):
        first = PAD + HALO + (k - 1) * 2
        s.hid_t[k * channels : (k + 1) * channels, :] = jnp.transpose(s.hid[first : first + rows, :].astype(BF16))
    s.hid2_t[...] = jnp.transpose(s.hid2[HALO : HALO + rows, :])

    col = lax.broadcasted_iota(jnp.int32, (rows, 1), 0)
    row = lax.broadcasted_iota(jnp.int32, (1, rows), 1)
    live = (col < own_count).astype(F32)
    first = z * rows
    offs_row = s.off[...]
    offs_col = jnp.transpose(jnp.broadcast_to(offs_row.astype(F32), (LANES, rows)))[:, 0:1].astype(jnp.int32)
    target_col = jnp.where(first + col - offs_col >= 0, col - offs_col, col + offs_col)
    target_row = jnp.where(first + row - offs_row >= 0, row - offs_row, row + offs_row)
    live_row = (row < own_count).astype(F32)
    band = jnp.where(target_col == row, live, 0.0) + jnp.where(target_row == col, live_row, 0.0)
    paired = jnp.dot(band.astype(BF16), own, preferred_element_type=F32)
    edge = lax.broadcasted_iota(jnp.int32, (1, HALO), 1)
    band_low = jnp.where(target_col == edge - HALO, live, 0.0)
    paired += jnp.dot(band_low.astype(BF16), s.emb_ext[0:HALO, :], preferred_element_type=F32)
    nextm.wait_recv()
    next_off = s.meta_next[0:1, 0:HALO]
    next_live = jnp.where(jnp.logical_and(has_high, edge < s.meta_next[1:2, 0:HALO]), 1.0, 0.0)
    band_high = jnp.where(rows + edge - next_off == col, next_live, 0.0)
    paired += jnp.dot(band_high.astype(BF16), s.emb_ext[HALO + rows :, :], preferred_element_type=F32)

    for copy in mpools:
        copy.wait_recv()

    def count_of(m):
        return own_count if m == 0 else s.meta_pool[m - 1, 1:2, 0:1]

    diag = col == row

    def scored(a_block, m):
        score = lax.dot_general(a_block, s.pool[m], (((1,), (1,)), ((), ())), preferred_element_type=F32)
        return jnp.exp(2.0 * score - 2.0)

    def summed(x, m):
        return jnp.sum(jnp.where(row < count_of(m), x, 0.0), axis=1, keepdims=True)

    x0 = jnp.where(diag, 0.0, scored(own, 0))
    s.xs[0] = x0.astype(BF16)
    denom = summed(x0, 0)
    for copies in pools:
        for copy in copies:
            copy.wait_recv()
    for m in range(1, n_batch):
        x = scored(own, m)
        s.xs[m] = x.astype(BF16)
        denom += summed(x, m)

    def set_rhs(a, a_live, a_denom):
        value = s.pool[a].astype(F32) * a_live
        s.rhs[a, :, 0:LANES] = value.astype(BF16)
        s.rhs[a, :, LANES : 2 * LANES] = (value / a_denom).astype(BF16)

    set_rhs(0, live, denom)
    if n_batch == 2:
        other_denom = summed(scored(s.pool[1], 0), 0)
        other_denom += summed(jnp.where(diag, 0.0, scored(s.pool[1], 1)), 1)
        set_rhs(1, (col < count_of(1)).astype(F32), other_denom)
    else:
        def one(a, carry):
            value = s.pool[a]
            den = jnp.zeros((rows, 1), F32)
            for m in range(n_batch):
                den += summed(jnp.where(jnp.logical_and(diag, a == m), 0.0, scored(value, m)), m)
            a_count = s.meta_pool[a - 1][1:2, 0:1]
            set_rhs(a, (col < a_count).astype(F32), den)
            return carry

        lax.fori_loop(1, n_batch, one, 0)
    acc = jnp.dot(s.xs[0], s.rhs[0], preferred_element_type=F32)
    for m in range(1, n_batch):
        acc += jnp.dot(s.xs[m], s.rhs[m], preferred_element_type=F32)
    unit = s.unit[HALO : HALO + rows, :]
    scale = s.scale[HALO : HALO + rows, :]
    grad_unit = 2.0 * (live * (acc[:, 0:LANES] / denom + acc[:, LANES:]) - paired)
    along = jnp.sum(unit * grad_unit, axis=1, keepdims=True)
    gf = ((grad_unit - unit * along) * scale).astype(BF16)
    gh = lax.dot_general(gf, s.proj[...], (((1,), (1,)), ((), ())), preferred_element_type=F32)
    gp = (gh * s.slope[HALO : HALO + rows, :]).astype(BF16)
    s.gp[...] = gp

    def with_bias(value):
        top = value[..., 0:body, :].astype(BF16)
        bias = value[..., body : body + PAD, :] + value[..., body + PAD :, :]
        high = bias.astype(BF16)
        return top, high, (bias - high.astype(F32)).astype(BF16)

    def put_p(ref, value):
        top, high, rest = with_bias(value)
        ref[..., 0:body, :] = top
        ref[..., body:, :] = jnp.concatenate([high, rest], axis=-2)

    ones = jnp.ones((HALO, rows), BF16)
    bias = jnp.dot(ones, s.gp[...], preferred_element_type=F32)
    proj = jnp.dot(s.hid2_t[...], gf, preferred_element_type=F32)
    high = bias.astype(BF16)
    rest = (bias - high.astype(F32)).astype(BF16)
    bias = jnp.concatenate([high[0:PAD], rest[0:PAD]], axis=0)
    for i in range(n_tm):
        for owner in range(2):
            begin = i * share + owner * body
            s.p_grads[owner, i, 0:body, :] = proj[begin : begin + body, :].astype(BF16)
            s.p_grads[owner, i, body:, 0:share] = bias[:, i * share : (i + 1) * share]
    p_rep = send(s.p_grads.at[other], s.p_rep, s.p_sem, (0,), {"rep": other})

    reps, bats, tms, gats = {}, {}, {}, {}

    def produce(c):
        value = jnp.dot(s.hid_t[c * span : (c + 1) * span, :], s.gp[...], preferred_element_type=F32)
        for owner in range(2):
            for i in range(n_tm):
                s.grads[c, owner, i, :, 0:share] = value[
                    owner * half : (owner + 1) * half, i * share : (i + 1) * share
                ].astype(BF16)
        reps[c] = send(s.grads.at[c, other], s.rep_in.at[c], s.rep_sem, (c,), {"rep": other})

    def over_batch(c):
        reps[c].wait_recv()
        s.part_one[c] = (s.grads[c, r].astype(F32) + s.rep_in[c].astype(F32)).astype(BF16)
        bats[c] = [
            send(
                s.part_one.at[c, :, pl.ds(pl.multiple_of(lax.rem(b + o, n_batch) * piece, piece), piece)],
                s.batch_in.at[c, o - 1], s.batch_sem, (c, o - 1), batch_at(o),
            )
            for o in range(1, n_batch)
        ]

    def over_tm(c):
        value = s.part_one[c, :, pl.ds(pl.multiple_of(b * piece, piece), piece)].astype(F32)
        for o in range(1, n_batch):
            bats[c][o - 1].wait_recv()
            value += s.batch_in[c, o - 1].astype(F32)
        s.part_two[c] = value.astype(BF16)
        tms[c] = [
            send(s.part_two.at[c, lax.rem(z + o, n_tm)], s.tm_in.at[c, o - 1], s.tm_sem, (c, o - 1), tm_at(o))
            for o in range(1, n_tm)
        ]

    def finish(c):
        value = s.part_two[c, z].astype(F32)
        for o in range(1, n_tm):
            tms[c][o - 1].wait_recv()
            value += s.tm_in[c, o - 1].astype(F32)
        at = pl.ds(pl.multiple_of(c * span + r * half + b * piece, piece), piece)
        s.final[at, :] = value.astype(BF16)
        mine = s.final.at[at]
        gats[c] = [send(mine, mine, s.gat_sem, (c, 0), {"rep": other})]
        for o in range(1, n_batch):
            gats[c].append(send(mine, mine, s.gat_sem, (c, 2 * o - 1), batch_at(o)))
            gats[c].append(send(mine, mine, s.gat_sem, (c, 2 * o), across_at(o)))

    p_copies = {}

    def p_over_tm():
        p_rep.wait_recv()
        put_p(s.p_one, s.p_grads[r].astype(F32) + s.p_rep[...].astype(F32))
        p_copies["tm"] = [
            send(s.p_one.at[lax.rem(z + o, n_tm)], s.p_tm.at[o - 1], s.p_tm_sem, (o - 1,), tm_at(o))
            for o in range(1, n_tm)
        ]

    def p_over_batch():
        value = s.p_one[z].astype(F32)
        for o in range(1, n_tm):
            p_copies["tm"][o - 1].wait_recv()
            value += s.p_tm[o - 1].astype(F32)
        put_p(s.p_part.at[b], value)
        p_copies["batch"] = [
            send(s.p_part.at[b], s.p_part.at[b], s.p_batch_sem, (o - 1,), batch_at(o)) for o in range(1, n_batch)
        ]

    def p_finish():
        for copy in p_copies["batch"]:
            copy.wait_recv()
        value = s.p_part[0].astype(F32)
        for i in range(1, n_batch):
            value += s.p_part[i].astype(F32)
        at = pl.ds(pl.multiple_of(3 * channels + r * extra, HALO), extra)
        put_p(s.final.at[at], value)
        mine = s.final.at[at]
        gats[chunks] = [send(mine, mine, s.p_gat_sem, (), {"rep": other})]

    for c in range(chunks):
        produce(c)
        if c == 0:
            p_over_tm()
        else:
            over_batch(c - 1)
    over_batch(chunks - 1)
    lag = 3
    for step in range(chunks + lag):
        if step < chunks:
            over_tm(step)
        if step == 1:
            p_over_batch()
        if step == 4:
            p_finish()
        if step >= lag:
            finish(step - lag)
    for c in sorted(gats):
        for copy in gats[c]:
            copy.wait_recv()
    s.sums_out[...] = s.final[...]
    store.wait()
    for copy in started:
        copy.wait_send()


def spread(share, emb_ref, sums_ref, emb_out, conv_out, bias_out, proj_out):
    channels = conv_out.shape[1]
    emb_out[...] = emb_ref[...]
    for k in range(3):
        conv_out[k] = sums_ref[k * channels : (k + 1) * channels, :].astype(F32)[:, 0:share]
    rest = 3 * channels
    body = share // 2
    for owner in range(2):
        begin = rest + owner * (body + HALO)
        proj_out[owner * body : (owner + 1) * body, :] = sums_ref[begin : begin + body, :].astype(F32)
    bias = sums_ref[rest + body : rest + body + HALO, :].astype(F32)
    bias_out[...] = (bias[0:PAD] + bias[PAD:])[0:1, 0:share]


def per_device(
    n_tm, n_batch,
    latents, session_ids, session_gain, session_shift, first_conv_weight, first_conv_bias,
    second_conv_weight, second_conv_bias, proj_weight, offsets, counts,
):
    rows, channels = latents.shape[1:]
    emb = proj_weight.shape[1]
    sessions = session_gain.shape[0]
    total = rows + 2 * HALO
    share = channels // n_tm
    span = channels // HALVES
    half = span // 2
    piece = half // n_batch
    chunks = 3 * HALVES
    extra = share // 2 + HALO
    out_rows = 3 * channels + 2 * extra
    vmem = pl.BlockSpec(memory_space=pltpu.VMEM)
    hbm = pl.BlockSpec(memory_space=pl.ANY)
    nb = n_batch - 1
    dma = pltpu.SemaphoreType.DMA
    inputs = ("lat", "sid", "cnt", "gain", "shift", "w1", "b1", "w2", "b2", "proj", "off")
    outputs = ("emb_out", "sums_out")
    scratch = {
        "lat": pltpu.VMEM((rows, channels), BF16),
        "sid": pltpu.SMEM((1,), jnp.int32),
        "cnt": pltpu.SMEM((1, 1), jnp.int32),
        "gain": pltpu.VMEM((sessions, channels), F32),
        "shift": pltpu.VMEM((sessions, channels), F32),
        "w1": pltpu.VMEM((3 * channels, channels), BF16),
        "b1": pltpu.VMEM((1, channels), F32),
        "w2": pltpu.VMEM((3 * channels, channels), BF16),
        "b2": pltpu.VMEM((1, channels), F32),
        "proj": pltpu.VMEM((channels, emb), BF16),
        "off": pltpu.VMEM((1, rows), jnp.int32),
        "halo": pltpu.VMEM((2, HALO, channels), BF16),
        "meta": pltpu.VMEM((8, LANES), jnp.int32),
        "meta_next": pltpu.VMEM((8, LANES), jnp.int32),
        "meta_pool": pltpu.VMEM((nb, 8, LANES), jnp.int32),
        "ext": pltpu.VMEM((total + 2 * PAD, channels), F32),
        "hid": pltpu.VMEM((total + 2 * PAD, channels), F32),
        "taps": pltpu.VMEM((total, 3 * channels), BF16),
        "pre": pltpu.VMEM((total, channels), F32),
        "slope": pltpu.VMEM((total, channels), F32),
        "hid2": pltpu.VMEM((total, channels), BF16),
        "unit": pltpu.VMEM((total, emb), F32),
        "scale": pltpu.VMEM((total, LANES), F32),
        "emb_ext": pltpu.VMEM((total, emb), BF16),
        "pool": pltpu.VMEM((n_batch, rows, emb), BF16),
        "xs": pltpu.VMEM((n_batch, rows, rows), BF16),
        "rhs": pltpu.VMEM((n_batch, rows, 2 * emb), BF16),
        "hid_t": pltpu.VMEM((3 * channels, rows), BF16),
        "hid2_t": pltpu.VMEM((channels, rows), BF16),
        "gp": pltpu.VMEM((rows, channels), BF16),
        "p_grads": pltpu.VMEM((2, n_tm, extra, LANES), BF16),
        "p_rep": pltpu.VMEM((n_tm, extra, LANES), BF16),
        "p_one": pltpu.VMEM((n_tm, extra, LANES), BF16),
        "p_tm": pltpu.VMEM((n_tm - 1, extra, LANES), BF16),
        "p_part": pltpu.VMEM((n_batch, extra, LANES), BF16),
        "grads": pltpu.VMEM((chunks, 2, n_tm, half, LANES), BF16),
        "rep_in": pltpu.VMEM((chunks, n_tm, half, LANES), BF16),
        "part_one": pltpu.VMEM((chunks, n_tm, half, LANES), BF16),
        "batch_in": pltpu.VMEM((chunks, nb, n_tm, piece, LANES), BF16),
        "part_two": pltpu.VMEM((chunks, n_tm, piece, LANES), BF16),
        "tm_in": pltpu.VMEM((chunks, n_tm - 1, piece, LANES), BF16),
        "final": pltpu.VMEM((out_rows, LANES), BF16),
        "load_sem": dma((len(inputs),)),
        "store_sem": dma,
        "halo_sem": dma((2, 2)),
        "meta_sem": dma((2, 1)),
        "mpool_sem": dma((2, nb)),
        "pool_sem": dma((2, INNER_BLOCKS + 2, nb)),
        "p_sem": dma((2, 1)),
        "p_tm_sem": dma((2, n_tm - 1)),
        "p_batch_sem": dma((2, nb)),
        "p_gat_sem": dma((2,)),
        "rep_sem": dma((2, chunks)),
        "batch_sem": dma((2, chunks, nb)),
        "tm_sem": dma((2, chunks, n_tm - 1)),
        "gat_sem": dma((2, chunks, 2 * nb + 1)),
    }
    names = tuple(n + "_hbm" for n in inputs) + outputs + tuple(scratch)
    embed, sums = pl.pallas_call(
        functools.partial(kernel, n_tm, n_batch, names),
        out_shape=(
            jax.ShapeDtypeStruct((rows, emb), BF16),
            jax.ShapeDtypeStruct((out_rows, LANES), BF16),
        ),
        in_specs=[hbm] * len(inputs),
        out_specs=(hbm, vmem),
        scratch_shapes=list(scratch.values()),
        compiler_params=pltpu.CompilerParams(
            collective_id=0, has_side_effects=True, vmem_limit_bytes=56 * 1024 * 1024
        ),
    )(
        latents[0], session_ids, counts, session_gain, session_shift,
        first_conv_weight.reshape(3 * channels, channels), first_conv_bias[None],
        second_conv_weight.reshape(3 * channels, channels), second_conv_bias[None],
        proj_weight, offsets,
    )
    embed, conv, bias, proj = pl.pallas_call(
        functools.partial(spread, share),
        out_shape=(
            jax.ShapeDtypeStruct((rows, emb), BF16),
            jax.ShapeDtypeStruct((3, channels, share), F32),
            jax.ShapeDtypeStruct((1, share), F32),
            jax.ShapeDtypeStruct((share, emb), F32),
        ),
        in_specs=[vmem, vmem],
        out_specs=(vmem, vmem, vmem, vmem),
    )(embed, sums)
    return embed[None], conv, bias[0], proj


def solution(mesh):
    return jax.shard_map(
        functools.partial(per_device, mesh.shape["tm"], mesh.shape["batch"]),
        mesh=mesh,
        in_specs=(
            P(("groups", "batch", "rep"), "tm", None),
            P(("groups", "batch", "rep")),
            P(),
            P(),
            P(),
            P(),
            P(),
            P(),
            P(),
            P(("groups", "batch", "rep"), "tm"),
            P(("groups", "batch", "rep"), "tm"),
        ),
        out_specs=(
            P(("groups", "batch", "rep"), "tm", None),
            P("groups", None, "tm"),
            P(("groups", "tm")),
            P(("groups", "tm"), None),
        ),
        check_vma=False,
    )
```

```python
import functools
import types

import jax
import jax.numpy as jnp
from jax import lax
from jax.experimental import pallas as pl
from jax.experimental.pallas import tpu as pltpu
from jax.sharding import PartitionSpec as P

HALO = 16
PAD = 8
LANES = 128
F32 = jnp.float32
BF16 = jnp.bfloat16
GELU_C = 0.7978845608028654
GELU_A = 0.044715
HALVES = 2
INNER_BLOCKS = 2
TM_FIRST = 1
LAG = 3


def gelu_parts(x):
    square = x * x
    th = jnp.tanh(GELU_C * x * (1.0 + GELU_A * square))
    half = 0.5 * (1.0 + th)
    slope = half + (0.5 * GELU_C) * x * (1.0 - th * th) * (1.0 + (3.0 * GELU_A) * square)
    return x * half, slope


def kernel(n_tm, n_batch, names, *refs):
    s = types.SimpleNamespace(**dict(zip(names, refs, strict=True)))
    rows, channels = s.lat.shape
    total = rows + 2 * HALO
    share = channels // n_tm
    span = channels // HALVES
    half = span // 2
    piece = half // n_batch
    chunks = 3 * HALVES
    extra = s.p_grads.shape[2]
    body = extra - HALO
    z = lax.axis_index("tm")
    b = lax.axis_index("batch")
    r = lax.axis_index("rep")
    other = 1 - r

    def tm_at(o):
        return {"tm": lax.rem(z + o, n_tm)}

    def batch_at(o):
        return {"batch": lax.rem(b + o, n_batch)}

    def across_at(o):
        return {"batch": lax.rem(b + o, n_batch), "rep": other}

    barrier = pltpu.get_barrier_semaphore()
    peers = [tm_at(o) for o in range(1, n_tm)] + [{"rep": other}]
    peers += [batch_at(o) for o in range(1, n_batch)] + [across_at(o) for o in range(1, n_batch)]
    for peer in peers:
        pl.semaphore_signal(barrier, inc=1, device_id=peer, device_id_type=pl.DeviceIdType.MESH)

    loads = {}
    for i, name in enumerate(("lat", "gain", "shift", "sid", "cnt", "off", "b1", "w1", "w2", "b2", "proj")):
        loads[name] = pltpu.make_async_copy(getattr(s, name + "_hbm"), getattr(s, name), s.load_sem.at[i])
        loads[name].start()

    pl.semaphore_wait(barrier, len(peers))
    started = []

    def send(src, dst, sems, index, peer):
        copy = pltpu.make_async_remote_copy(
            src_ref=src, dst_ref=dst, send_sem=sems.at[(0,) + index], recv_sem=sems.at[(1,) + index],
            device_id=peer, device_id_type=pl.DeviceIdType.MESH,
        )
        copy.start()
        started.append(copy)
        return copy

    low = send(s.lat_hbm.at[pl.ds(rows - HALO, HALO)], s.halo.at[0], s.halo_sem, (0,), tm_at(1))
    high = send(s.lat_hbm.at[pl.ds(0, HALO)], s.halo.at[1], s.halo_sem, (1,), tm_at(n_tm - 1))

    s.ext[0:PAD, :] = jnp.zeros((PAD, channels), F32)
    s.ext[PAD + total :, :] = jnp.zeros((PAD, channels), F32)
    s.hid[0:PAD, :] = jnp.zeros((PAD, channels), F32)
    s.hid[PAD + total :, :] = jnp.zeros((PAD, channels), F32)
    has_low = z > 0
    has_high = z < n_tm - 1

    for name in ("gain", "shift", "sid", "cnt", "off"):
        loads[name].wait()
    own_count = s.cnt[0, 0]
    s.meta[0:1, :] = s.off[0:1, 0:LANES]
    s.meta[1:2, :] = jnp.full((1, LANES), own_count, jnp.int32)
    s.meta[2:8, :] = jnp.zeros((6, LANES), jnp.int32)
    nextm = send(s.meta, s.meta_next, s.meta_sem, (0,), tm_at(n_tm - 1))
    mpools = [send(s.meta, s.meta_pool.at[o - 1], s.mpool_sem, (o - 1,), batch_at(o)) for o in range(1, n_batch)]
    pick = lax.broadcasted_iota(jnp.int32, s.gain.shape, 0) == s.sid[0]
    gain = jnp.sum(jnp.where(pick, s.gain[...], 0.0), axis=0, keepdims=True)
    shift = jnp.sum(jnp.where(pick, s.shift[...], 0.0), axis=0, keepdims=True)

    def based(block):
        return (block.astype(F32) * gain + shift).astype(BF16).astype(F32)

    def gather_taps(source, dilation, begin, count):
        for k in range(3):
            first = PAD + begin + (k - 1) * dilation
            s.taps[begin : begin + count, k * channels : (k + 1) * channels] = source[first : first + count, :].astype(
                BF16
            )

    def first_hidden(begin, count):
        x = s.pre[begin : begin + count, :] + s.b1[...]
        value = 0.5 * x * (1.0 + jnp.tanh(GELU_C * x * (1.0 + GELU_A * x * x)))
        return (s.ext[PAD + begin : PAD + begin + count, :] + value).astype(BF16).astype(F32)

    def second_hidden(begin, count):
        value, deriv = gelu_parts(s.pre[begin : begin + count, :] + s.b2[...])
        s.slope[begin : begin + count, :] = deriv
        hid = (s.hid[PAD + begin : PAD + begin + count, :] + value).astype(BF16)
        s.hid2[begin : begin + count, :] = hid
        feats = jnp.dot(hid, s.proj[...], preferred_element_type=F32)
        scale = lax.rsqrt(jnp.sum(feats * feats, axis=1, keepdims=True) + 1e-06)
        unit = feats * scale
        s.unit[begin : begin + count, :] = unit
        s.scale[begin : begin + count, :] = jnp.broadcast_to(scale, (count, LANES))
        s.emb_ext[begin : begin + count, :] = unit.astype(BF16)

    pools = []

    def send_pool(first, count):
        at = pl.ds(first, count)
        i = len(pools)
        s.pool[0, first : first + count, :] = s.emb_ext[HALO + first : HALO + first + count, :]
        pools.append([
            send(s.pool.at[0, at], s.pool.at[o, at], s.pool_sem, (i, o - 1), batch_at(o)) for o in range(1, n_batch)
        ])

    loads["lat"].wait()
    s.ext[PAD + HALO : PAD + HALO + rows, :] = based(s.lat[...])
    near, near_rows = HALO + PAD, rows - 2 * PAD
    gather_taps(s.ext, 1, near, near_rows)
    loads["b1"].wait()
    loads["w1"].wait()
    s.pre[near : near + near_rows, :] = jnp.dot(
        s.taps[near : near + near_rows, :], s.w1[...], preferred_element_type=F32
    )
    s.hid[PAD + near : PAD + near + near_rows, :] = first_hidden(near, near_rows)
    block = (rows - 2 * HALO) // INNER_BLOCKS
    for name in ("w2", "b2", "proj"):
        loads[name].wait()
    for i in range(INNER_BLOCKS):
        begin = 2 * HALO + i * block
        gather_taps(s.hid, 2, begin, block)
        s.pre[begin : begin + block, :] = jnp.dot(
            s.taps[begin : begin + block, :], s.w2[...], preferred_element_type=F32
        )
        second_hidden(begin, block)
        send_pool(begin - HALO, block)

    edge_rows = 2 * HALO
    last = total - edge_rows
    low.wait_recv()
    high.wait_recv()
    s.ext[PAD : PAD + HALO, :] = jnp.where(has_low, based(s.halo[0]), 0.0)
    s.ext[PAD + HALO + rows : PAD + total, :] = jnp.where(has_high, based(s.halo[1]), 0.0)

    def conv_ends(source, dilation, weight):
        gather_taps(source, dilation, 0, edge_rows)
        gather_taps(source, dilation, last, edge_rows)
        ends = jnp.concatenate([s.taps[0:edge_rows, :], s.taps[last:, :]], axis=0)
        ends = jnp.dot(ends, weight[...], preferred_element_type=F32)
        s.pre[0:edge_rows, :] = ends[0:edge_rows, :]
        s.pre[last:, :] = ends[edge_rows:, :]

    conv_ends(s.ext, 1, s.w1)
    at = lax.broadcasted_iota(jnp.int32, (edge_rows, 1), 0)
    s.hid[PAD : PAD + edge_rows, :] = jnp.where(
        jnp.logical_or(has_low, at >= HALO), first_hidden(0, edge_rows), 0.0
    )
    s.hid[PAD + last : PAD + total, :] = jnp.where(
        jnp.logical_or(has_high, at < HALO), first_hidden(last, edge_rows), 0.0
    )
    conv_ends(s.hid, 2, s.w2)
    second_hidden(0, edge_rows)
    second_hidden(last, edge_rows)
    send_pool(0, HALO)
    send_pool(rows - HALO, HALO)
    own = s.pool[0]
    store = pltpu.make_async_copy(s.pool.at[0], s.emb_out, s.store_sem)
    store.start()

    for k in range(3):
        first = PAD + HALO + (k - 1) * 2
        s.hid_t[k * channels : (k + 1) * channels, :] = jnp.transpose(s.hid[first : first + rows, :].astype(BF16))
    s.hid2_t[...] = jnp.transpose(s.hid2[HALO : HALO + rows, :])

    col = lax.broadcasted_iota(jnp.int32, (rows, 1), 0)
    row = lax.broadcasted_iota(jnp.int32, (1, rows), 1)
    live = (col < own_count).astype(F32)
    first = z * rows
    offs_row = s.off[...]
    offs_col = jnp.transpose(jnp.broadcast_to(offs_row.astype(F32), (LANES, rows)))[:, 0:1].astype(jnp.int32)
    target_col = jnp.where(first + col - offs_col >= 0, col - offs_col, col + offs_col)
    target_row = jnp.where(first + row - offs_row >= 0, row - offs_row, row + offs_row)
    live_row = (row < own_count).astype(F32)
    band = jnp.where(target_col == row, live, 0.0) + jnp.where(target_row == col, live_row, 0.0)
    paired = jnp.dot(band.astype(BF16), own, preferred_element_type=F32)
    edge = lax.broadcasted_iota(jnp.int32, (1, HALO), 1)
    band_low = jnp.where(target_col == edge - HALO, live, 0.0)
    paired += jnp.dot(band_low.astype(BF16), s.emb_ext[0:HALO, :], preferred_element_type=F32)
    nextm.wait_recv()
    next_off = s.meta_next[0:1, 0:HALO]
    next_live = jnp.where(jnp.logical_and(has_high, edge < s.meta_next[1:2, 0:HALO]), 1.0, 0.0)
    band_high = jnp.where(rows + edge - next_off == col, next_live, 0.0)
    paired += jnp.dot(band_high.astype(BF16), s.emb_ext[HALO + rows :, :], preferred_element_type=F32)

    for copy in mpools:
        copy.wait_recv()

    def count_of(m):
        return own_count if m == 0 else s.meta_pool[m - 1, 1:2, 0:1]

    diag = col == row

    def scored(a_block, m):
        score = lax.dot_general(a_block, s.pool[m], (((1,), (1,)), ((), ())), preferred_element_type=F32)
        return jnp.exp(2.0 * score - 2.0)

    def summed(x, m):
        return jnp.sum(jnp.where(row < count_of(m), x, 0.0), axis=1, keepdims=True)

    x0 = jnp.where(diag, 0.0, scored(own, 0))
    s.xs[0] = x0.astype(BF16)
    denom = summed(x0, 0)
    for copies in pools:
        for copy in copies:
            copy.wait_recv()
    for m in range(1, n_batch):
        x = scored(own, m)
        s.xs[m] = x.astype(BF16)
        denom += summed(x, m)

    def set_rhs(a, a_live, a_denom):
        value = s.pool[a].astype(F32) * a_live
        s.rhs[a, :, 0:LANES] = value.astype(BF16)
        s.rhs[a, :, LANES : 2 * LANES] = (value / a_denom).astype(BF16)

    set_rhs(0, live, denom)
    if n_batch == 2:
        other_denom = summed(scored(s.pool[1], 0), 0)
        other_denom += summed(jnp.where(diag, 0.0, scored(s.pool[1], 1)), 1)
        set_rhs(1, (col < count_of(1)).astype(F32), other_denom)
    else:
        def one(a, carry):
            value = s.pool[a]
            den = jnp.zeros((rows, 1), F32)
            for m in range(n_batch):
                den += summed(jnp.where(jnp.logical_and(diag, a == m), 0.0, scored(value, m)), m)
            a_count = s.meta_pool[a - 1][1:2, 0:1]
            set_rhs(a, (col < a_count).astype(F32), den)
            return carry

        lax.fori_loop(1, n_batch, one, 0)
    acc = jnp.dot(s.xs[0], s.rhs[0], preferred_element_type=F32)
    for m in range(1, n_batch):
        acc += jnp.dot(s.xs[m], s.rhs[m], preferred_element_type=F32)
    unit = s.unit[HALO : HALO + rows, :]
    scale = s.scale[HALO : HALO + rows, :]
    grad_unit = 2.0 * (live * (acc[:, 0:LANES] / denom + acc[:, LANES:]) - paired)
    along = jnp.sum(unit * grad_unit, axis=1, keepdims=True)
    gf = ((grad_unit - unit * along) * scale).astype(BF16)
    gh = lax.dot_general(gf, s.proj[...], (((1,), (1,)), ((), ())), preferred_element_type=F32)
    gp = (gh * s.slope[HALO : HALO + rows, :]).astype(BF16)
    s.gp[...] = gp

    def with_bias(value):
        top = value[..., 0:body, :].astype(BF16)
        bias = value[..., body : body + PAD, :] + value[..., body + PAD :, :]
        high = bias.astype(BF16)
        return top, high, (bias - high.astype(F32)).astype(BF16)

    def put_p(ref, value):
        top, high, rest = with_bias(value)
        ref[..., 0:body, :] = top
        ref[..., body:, :] = jnp.concatenate([high, rest], axis=-2)

    reps, bats, tms, gats = {}, {}, {}, {}

    def produce(c):
        value = jnp.dot(s.hid_t[c * span : (c + 1) * span, :], s.gp[...], preferred_element_type=F32)
        for owner in range(2):
            for i in range(n_tm):
                s.grads[c, owner, i, :, 0:share] = value[
                    owner * half : (owner + 1) * half, i * share : (i + 1) * share
                ].astype(BF16)
        reps[c] = send(s.grads.at[c, other], s.rep_in.at[c], s.rep_sem, (c,), {"rep": other})

    def over_batch(c):
        reps[c].wait_recv()
        s.part_one[c] = (s.grads[c, r].astype(F32) + s.rep_in[c].astype(F32)).astype(BF16)
        bats[c] = [
            send(
                s.part_one.at[c, :, pl.ds(pl.multiple_of(lax.rem(b + o, n_batch) * piece, piece), piece)],
                s.batch_in.at[c, o - 1], s.batch_sem, (c, o - 1), batch_at(o),
            )
            for o in range(1, n_batch)
        ]

    def over_tm(c):
        value = s.part_one[c, :, pl.ds(pl.multiple_of(b * piece, piece), piece)].astype(F32)
        for o in range(1, n_batch):
            bats[c][o - 1].wait_recv()
            value += s.batch_in[c, o - 1].astype(F32)
        s.part_two[c] = value.astype(BF16)
        tms[c] = [
            send(s.part_two.at[c, lax.rem(z + o, n_tm)], s.tm_in.at[c, o - 1], s.tm_sem, (c, o - 1), tm_at(o))
            for o in range(1, n_tm)
        ]

    def finish(c):
        value = s.part_two[c, z].astype(F32)
        for o in range(1, n_tm):
            tms[c][o - 1].wait_recv()
            value += s.tm_in[c, o - 1].astype(F32)
        at = pl.ds(pl.multiple_of(c * span + r * half + b * piece, piece), piece)
        s.final[at, :] = value.astype(BF16)
        mine = s.final.at[at]
        gats[c] = [send(mine, mine, s.gat_sem, (c, 0), {"rep": other})]
        for o in range(1, n_batch):
            gats[c].append(send(mine, mine, s.gat_sem, (c, 2 * o - 1), batch_at(o)))
            gats[c].append(send(mine, mine, s.gat_sem, (c, 2 * o), across_at(o)))

    p_copies = {}

    def make_p():
        ones = jnp.ones((HALO, rows), BF16)
        bias = jnp.dot(ones, s.gp[...], preferred_element_type=F32)
        proj = jnp.dot(s.hid2_t[...], gf, preferred_element_type=F32)
        high = bias.astype(BF16)
        rest = (bias - high.astype(F32)).astype(BF16)
        bias = jnp.concatenate([high[0:PAD], rest[0:PAD]], axis=0)
        for i in range(n_tm):
            for owner in range(2):
                begin = i * share + owner * body
                s.p_grads[owner, i, 0:body, :] = proj[begin : begin + body, :].astype(BF16)
                s.p_grads[owner, i, body:, 0:share] = bias[:, i * share : (i + 1) * share]
        p_copies["rep"] = send(s.p_grads.at[other], s.p_rep, s.p_sem, (0,), {"rep": other})

    def p_over_tm():
        p_copies["rep"].wait_recv()
        put_p(s.p_one, s.p_grads[r].astype(F32) + s.p_rep[...].astype(F32))
        p_copies["tm"] = [
            send(s.p_one.at[lax.rem(z + o, n_tm)], s.p_tm.at[o - 1], s.p_tm_sem, (o - 1,), tm_at(o))
            for o in range(1, n_tm)
        ]

    def p_over_batch():
        value = s.p_one[z].astype(F32)
        for o in range(1, n_tm):
            p_copies["tm"][o - 1].wait_recv()
            value += s.p_tm[o - 1].astype(F32)
        put_p(s.p_part.at[b], value)
        p_copies["batch"] = [
            send(s.p_part.at[b], s.p_part.at[b], s.p_batch_sem, (o - 1,), batch_at(o)) for o in range(1, n_batch)
        ]

    def p_finish():
        for copy in p_copies["batch"]:
            copy.wait_recv()
        value = s.p_part[0].astype(F32)
        for i in range(1, n_batch):
            value += s.p_part[i].astype(F32)
        at = pl.ds(pl.multiple_of(3 * channels + r * extra, HALO), extra)
        put_p(s.final.at[at], value)
        mine = s.final.at[at]
        gats[chunks] = [send(mine, mine, s.p_gat_sem, (), {"rep": other})]

    def tm_first(c):
        reps[c].wait_recv()
        s.part_one[c] = (s.grads[c, r].astype(F32) + s.rep_in[c].astype(F32)).astype(BF16)
        tms[c] = [
            send(s.part_one.at[c, lax.rem(z + o, n_tm)], s.zf_tm.at[c, o - 1], s.tm_sem, (c, o - 1), tm_at(o))
            for o in range(1, n_tm)
        ]

    def then_batch(c):
        value = s.part_one[c, z].astype(F32)
        for o in range(1, n_tm):
            tms[c][o - 1].wait_recv()
            value += s.zf_tm[c, o - 1].astype(F32)
        s.zf_part[c, b] = value.astype(BF16)
        mine = s.zf_part.at[c, b]
        bats[c] = [send(mine, mine, s.batch_sem, (c, o - 1), batch_at(o)) for o in range(1, n_batch)]

    def finish_tm_first(c):
        for copy in bats[c]:
            copy.wait_recv()
        value = s.zf_part[c, 0].astype(F32)
        for i in range(1, n_batch):
            value += s.zf_part[c, i].astype(F32)
        at = pl.ds(pl.multiple_of(c * span + r * half, half), half)
        s.final[at, :] = value.astype(BF16)
        mine = s.final.at[at]
        gats[c] = [send(mine, mine, s.gat_sem, (c, 0), {"rep": other})]

    ring = list(range(TM_FIRST))
    line = list(range(TM_FIRST, chunks))
    produce(line[0])
    for c in ring:
        produce(c)
    if not ring:
        produce(line[1])
    over_batch(line[0])
    for c in ring:
        tm_first(c)
    if ring:
        produce(line[1])
    make_p()
    over_batch(line[1])
    produce(line[2])
    p_over_tm()
    for i in range(3, len(line)):
        produce(line[i])
        over_batch(line[i - 1])
    over_batch(line[-1])
    for step in range(len(line) + LAG):
        if step < len(line):
            over_tm(line[step])
        if step == 2:
            for c in ring:
                then_batch(c)
            p_over_batch()
        if step == len(line) - 1:
            for c in ring:
                finish_tm_first(c)
            p_finish()
        if step >= LAG:
            finish(line[step - LAG])
    stores = [store]
    for c in [*ring, chunks, *line]:
        for copy in gats[c]:
            copy.wait_recv()
        at = pl.ds(c * span, span) if c < chunks else pl.ds(3 * channels, 2 * extra)
        stores.append(pltpu.make_async_copy(s.final.at[at], s.sums_out.at[at], s.sums_sem.at[c]))
        stores[-1].start()
    for copy in stores:
        copy.wait()
    for copy in started:
        copy.wait_send()


def spread(share, emb_ref, sums_ref, emb_out, conv_out, bias_out, proj_out):
    channels = conv_out.shape[1]
    emb_out[...] = emb_ref[...]
    for k in range(3):
        conv_out[k] = sums_ref[k * channels : (k + 1) * channels, :].astype(F32)[:, 0:share]
    rest = 3 * channels
    body = share // 2
    for owner in range(2):
        begin = rest + owner * (body + HALO)
        proj_out[owner * body : (owner + 1) * body, :] = sums_ref[begin : begin + body, :].astype(F32)
    bias = sums_ref[rest + body : rest + body + HALO, :].astype(F32)
    bias_out[...] = (bias[0:PAD] + bias[PAD:])[0:1, 0:share]


def per_device(
    n_tm, n_batch,
    latents, session_ids, session_gain, session_shift, first_conv_weight, first_conv_bias,
    second_conv_weight, second_conv_bias, proj_weight, offsets, counts,
):
    rows, channels = latents.shape[1:]
    emb = proj_weight.shape[1]
    sessions = session_gain.shape[0]
    total = rows + 2 * HALO
    share = channels // n_tm
    span = channels // HALVES
    half = span // 2
    piece = half // n_batch
    chunks = 3 * HALVES
    extra = share // 2 + HALO
    out_rows = 3 * channels + 2 * extra
    vmem = pl.BlockSpec(memory_space=pltpu.VMEM)
    hbm = pl.BlockSpec(memory_space=pl.ANY)
    nb = n_batch - 1
    dma = pltpu.SemaphoreType.DMA
    inputs = ("lat", "sid", "cnt", "gain", "shift", "w1", "b1", "w2", "b2", "proj", "off")
    outputs = ("emb_out", "sums_out")
    scratch = {
        "lat": pltpu.VMEM((rows, channels), BF16),
        "sid": pltpu.SMEM((1,), jnp.int32),
        "cnt": pltpu.SMEM((1, 1), jnp.int32),
        "gain": pltpu.VMEM((sessions, channels), F32),
        "shift": pltpu.VMEM((sessions, channels), F32),
        "w1": pltpu.VMEM((3 * channels, channels), BF16),
        "b1": pltpu.VMEM((1, channels), F32),
        "w2": pltpu.VMEM((3 * channels, channels), BF16),
        "b2": pltpu.VMEM((1, channels), F32),
        "proj": pltpu.VMEM((channels, emb), BF16),
        "off": pltpu.VMEM((1, rows), jnp.int32),
        "halo": pltpu.VMEM((2, HALO, channels), BF16),
        "meta": pltpu.VMEM((8, LANES), jnp.int32),
        "meta_next": pltpu.VMEM((8, LANES), jnp.int32),
        "meta_pool": pltpu.VMEM((nb, 8, LANES), jnp.int32),
        "ext": pltpu.VMEM((total + 2 * PAD, channels), F32),
        "hid": pltpu.VMEM((total + 2 * PAD, channels), F32),
        "taps": pltpu.VMEM((total, 3 * channels), BF16),
        "pre": pltpu.VMEM((total, channels), F32),
        "slope": pltpu.VMEM((total, channels), F32),
        "hid2": pltpu.VMEM((total, channels), BF16),
        "unit": pltpu.VMEM((total, emb), F32),
        "scale": pltpu.VMEM((total, LANES), F32),
        "emb_ext": pltpu.VMEM((total, emb), BF16),
        "pool": pltpu.VMEM((n_batch, rows, emb), BF16),
        "xs": pltpu.VMEM((n_batch, rows, rows), BF16),
        "rhs": pltpu.VMEM((n_batch, rows, 2 * emb), BF16),
        "hid_t": pltpu.VMEM((3 * channels, rows), BF16),
        "hid2_t": pltpu.VMEM((channels, rows), BF16),
        "gp": pltpu.VMEM((rows, channels), BF16),
        "p_grads": pltpu.VMEM((2, n_tm, extra, LANES), BF16),
        "p_rep": pltpu.VMEM((n_tm, extra, LANES), BF16),
        "p_one": pltpu.VMEM((n_tm, extra, LANES), BF16),
        "p_tm": pltpu.VMEM((n_tm - 1, extra, LANES), BF16),
        "p_part": pltpu.VMEM((n_batch, extra, LANES), BF16),
        "grads": pltpu.VMEM((chunks, 2, n_tm, half, LANES), BF16),
        "rep_in": pltpu.VMEM((chunks, n_tm, half, LANES), BF16),
        "part_one": pltpu.VMEM((chunks, n_tm, half, LANES), BF16),
        "batch_in": pltpu.VMEM((chunks, nb, n_tm, piece, LANES), BF16),
        "part_two": pltpu.VMEM((chunks, n_tm, piece, LANES), BF16),
        "tm_in": pltpu.VMEM((chunks, n_tm - 1, piece, LANES), BF16),
        "zf_tm": pltpu.VMEM((max(TM_FIRST, 1), n_tm - 1, half, LANES), BF16),
        "zf_part": pltpu.VMEM((max(TM_FIRST, 1), n_batch, half, LANES), BF16),
        "final": pltpu.VMEM((out_rows, LANES), BF16),
        "load_sem": dma((len(inputs),)),
        "store_sem": dma,
        "sums_sem": dma((chunks + 1,)),
        "halo_sem": dma((2, 2)),
        "meta_sem": dma((2, 1)),
        "mpool_sem": dma((2, nb)),
        "pool_sem": dma((2, INNER_BLOCKS + 2, nb)),
        "p_sem": dma((2, 1)),
        "p_tm_sem": dma((2, n_tm - 1)),
        "p_batch_sem": dma((2, nb)),
        "p_gat_sem": dma((2,)),
        "rep_sem": dma((2, chunks)),
        "batch_sem": dma((2, chunks, nb)),
        "tm_sem": dma((2, chunks, n_tm - 1)),
        "gat_sem": dma((2, chunks, 2 * nb + 1)),
    }
    names = tuple(n + "_hbm" for n in inputs) + outputs + tuple(scratch)
    embed, sums = pl.pallas_call(
        functools.partial(kernel, n_tm, n_batch, names),
        out_shape=(
            jax.ShapeDtypeStruct((rows, emb), BF16),
            jax.ShapeDtypeStruct((out_rows, LANES), BF16),
        ),
        in_specs=[hbm] * len(inputs),
        out_specs=(hbm, hbm),
        scratch_shapes=list(scratch.values()),
        compiler_params=pltpu.CompilerParams(
            collective_id=0, has_side_effects=True, vmem_limit_bytes=56 * 1024 * 1024
        ),
    )(
        latents[0], session_ids, counts, session_gain, session_shift,
        first_conv_weight.reshape(3 * channels, channels), first_conv_bias[None],
        second_conv_weight.reshape(3 * channels, channels), second_conv_bias[None],
        proj_weight, offsets,
    )
    embed, conv, bias, proj = pl.pallas_call(
        functools.partial(spread, share),
        out_shape=(
            jax.ShapeDtypeStruct((rows, emb), BF16),
            jax.ShapeDtypeStruct((3, channels, share), F32),
            jax.ShapeDtypeStruct((1, share), F32),
            jax.ShapeDtypeStruct((share, emb), F32),
        ),
        in_specs=[vmem, vmem],
        out_specs=(vmem, vmem, vmem, vmem),
    )(embed, sums)
    return embed[None], conv, bias[0], proj


def solution(mesh):
    return jax.shard_map(
        functools.partial(per_device, mesh.shape["tm"], mesh.shape["batch"]),
        mesh=mesh,
        in_specs=(
            P(("groups", "batch", "rep"), "tm", None),
            P(("groups", "batch", "rep")),
            P(),
            P(),
            P(),
            P(),
            P(),
            P(),
            P(),
            P(("groups", "batch", "rep"), "tm"),
            P(("groups", "batch", "rep"), "tm"),
        ),
        out_specs=(
            P(("groups", "batch", "rep"), "tm", None),
            P("groups", None, "tm"),
            P(("groups", "tm")),
            P(("groups", "tm"), None),
        ),
        check_vma=False,
    )
```

```python
import functools
import types

import jax
import jax.numpy as jnp
from jax import lax
from jax.experimental import pallas as pl
from jax.experimental.pallas import tpu as pltpu
from jax.sharding import PartitionSpec as P

HALO = 16
PAD = 8
LANES = 128
F32 = jnp.float32
BF16 = jnp.bfloat16
GELU_C = 0.7978845608028654
GELU_A = 0.044715
HALVES = 2
INNER_BLOCKS = 2
TM_FIRST = 1
LAG = 3


def gelu_parts(x):
    square = x * x
    th = jnp.tanh(GELU_C * x * (1.0 + GELU_A * square))
    half = 0.5 * (1.0 + th)
    slope = half + (0.5 * GELU_C) * x * (1.0 - th * th) * (1.0 + (3.0 * GELU_A) * square)
    return x * half, slope


def kernel(n_tm, n_batch, names, *refs):
    s = types.SimpleNamespace(**dict(zip(names, refs, strict=True)))
    rows, channels = s.lat.shape
    total = rows + 2 * HALO
    share = channels // n_tm
    span = channels // HALVES
    half = span // 2
    piece = half // n_batch
    chunks = 3 * HALVES
    extra = s.p_grads.shape[2]
    body = extra - HALO
    z = lax.axis_index("tm")
    b = lax.axis_index("batch")
    r = lax.axis_index("rep")
    other = 1 - r

    def tm_at(o):
        return {"tm": lax.rem(z + o, n_tm)}

    def batch_at(o):
        return {"batch": lax.rem(b + o, n_batch)}

    def across_at(o):
        return {"batch": lax.rem(b + o, n_batch), "rep": other}

    barrier = pltpu.get_barrier_semaphore()
    peers = [tm_at(o) for o in range(1, n_tm)] + [{"rep": other}]
    peers += [batch_at(o) for o in range(1, n_batch)] + [across_at(o) for o in range(1, n_batch)]
    for peer in peers:
        pl.semaphore_signal(barrier, inc=1, device_id=peer, device_id_type=pl.DeviceIdType.MESH)

    loads = {}
    for i, name in enumerate(("lat", "gain", "shift", "sid", "cnt", "off", "b1", "w1", "w2", "b2", "proj")):
        loads[name] = pltpu.make_async_copy(getattr(s, name + "_hbm"), getattr(s, name), s.load_sem.at[i])
        if name not in ("w2", "b2", "proj"):
            loads[name].start()

    pl.semaphore_wait(barrier, len(peers))
    started = []

    def send(src, dst, sems, index, peer):
        copy = pltpu.make_async_remote_copy(
            src_ref=src, dst_ref=dst, send_sem=sems.at[(0,) + index], recv_sem=sems.at[(1,) + index],
            device_id=peer, device_id_type=pl.DeviceIdType.MESH,
        )
        copy.start()
        started.append(copy)
        return copy

    low = send(s.lat_hbm.at[pl.ds(rows - HALO, HALO)], s.halo.at[0], s.halo_sem, (0,), tm_at(1))
    high = send(s.lat_hbm.at[pl.ds(0, HALO)], s.halo.at[1], s.halo_sem, (1,), tm_at(n_tm - 1))

    s.ext[0:PAD, :] = jnp.zeros((PAD, channels), F32)
    s.ext[PAD + total :, :] = jnp.zeros((PAD, channels), F32)
    s.hid[0:PAD, :] = jnp.zeros((PAD, channels), F32)
    s.hid[PAD + total :, :] = jnp.zeros((PAD, channels), F32)
    has_low = z > 0
    has_high = z < n_tm - 1

    for name in ("gain", "shift", "sid", "cnt", "off"):
        loads[name].wait()
    own_count = s.cnt[0, 0]
    s.meta[0:1, :] = s.off[0:1, 0:LANES]
    s.meta[1:2, :] = jnp.full((1, LANES), own_count, jnp.int32)
    s.meta[2:8, :] = jnp.zeros((6, LANES), jnp.int32)
    nextm = send(s.meta, s.meta_next, s.meta_sem, (0,), tm_at(n_tm - 1))
    mpools = [send(s.meta, s.meta_pool.at[o - 1], s.mpool_sem, (o - 1,), batch_at(o)) for o in range(1, n_batch)]
    pick = lax.broadcasted_iota(jnp.int32, s.gain.shape, 0) == s.sid[0]
    gain = jnp.sum(jnp.where(pick, s.gain[...], 0.0), axis=0, keepdims=True)
    shift = jnp.sum(jnp.where(pick, s.shift[...], 0.0), axis=0, keepdims=True)

    def based(block):
        return (block.astype(F32) * gain + shift).astype(BF16).astype(F32)

    def gather_taps(source, dilation, begin, count):
        for k in range(3):
            first = PAD + begin + (k - 1) * dilation
            s.taps[begin : begin + count, k * channels : (k + 1) * channels] = source[first : first + count, :].astype(
                BF16
            )

    def first_hidden(begin, count):
        x = s.pre[begin : begin + count, :] + s.b1[...]
        value = 0.5 * x * (1.0 + jnp.tanh(GELU_C * x * (1.0 + GELU_A * x * x)))
        return (s.ext[PAD + begin : PAD + begin + count, :] + value).astype(BF16).astype(F32)

    def second_hidden(begin, count):
        value, deriv = gelu_parts(s.pre[begin : begin + count, :] + s.b2[...])
        s.slope[begin : begin + count, :] = deriv
        hid = (s.hid[PAD + begin : PAD + begin + count, :] + value).astype(BF16)
        s.hid2[begin : begin + count, :] = hid
        feats = jnp.dot(hid, s.proj[...], preferred_element_type=F32)
        scale = lax.rsqrt(jnp.sum(feats * feats, axis=1, keepdims=True) + 1e-06)
        unit = feats * scale
        s.unit[begin : begin + count, :] = unit
        s.scale[begin : begin + count, :] = jnp.broadcast_to(scale, (count, LANES))
        s.emb_ext[begin : begin + count, :] = unit.astype(BF16)

    pools = []

    def send_pool(first, count):
        at = pl.ds(first, count)
        i = len(pools)
        s.pool[0, first : first + count, :] = s.emb_ext[HALO + first : HALO + first + count, :]
        pools.append([
            send(s.pool.at[0, at], s.pool.at[o, at], s.pool_sem, (i, o - 1), batch_at(o)) for o in range(1, n_batch)
        ])

    loads["lat"].wait()
    for name in ("w2", "b2", "proj"):
        loads[name].start()
    s.ext[PAD + HALO : PAD + HALO + rows, :] = based(s.lat[...])
    near, near_rows = HALO + PAD, rows - 2 * PAD
    gather_taps(s.ext, 1, near, near_rows)
    loads["b1"].wait()
    loads["w1"].wait()
    s.pre[near : near + near_rows, :] = jnp.dot(
        s.taps[near : near + near_rows, :], s.w1[...], preferred_element_type=F32
    )
    s.hid[PAD + near : PAD + near + near_rows, :] = first_hidden(near, near_rows)
    block = (rows - 2 * HALO) // INNER_BLOCKS
    for name in ("w2", "b2", "proj"):
        loads[name].wait()
    for i in range(INNER_BLOCKS):
        begin = 2 * HALO + i * block
        gather_taps(s.hid, 2, begin, block)
        s.pre[begin : begin + block, :] = jnp.dot(
            s.taps[begin : begin + block, :], s.w2[...], preferred_element_type=F32
        )
        second_hidden(begin, block)
        send_pool(begin - HALO, block)

    edge_rows = 2 * HALO
    last = total - edge_rows
    low.wait_recv()
    high.wait_recv()
    s.ext[PAD : PAD + HALO, :] = jnp.where(has_low, based(s.halo[0]), 0.0)
    s.ext[PAD + HALO + rows : PAD + total, :] = jnp.where(has_high, based(s.halo[1]), 0.0)

    def conv_ends(source, dilation, weight):
        gather_taps(source, dilation, 0, edge_rows)
        gather_taps(source, dilation, last, edge_rows)
        ends = jnp.concatenate([s.taps[0:edge_rows, :], s.taps[last:, :]], axis=0)
        ends = jnp.dot(ends, weight[...], preferred_element_type=F32)
        s.pre[0:edge_rows, :] = ends[0:edge_rows, :]
        s.pre[last:, :] = ends[edge_rows:, :]

    conv_ends(s.ext, 1, s.w1)
    at = lax.broadcasted_iota(jnp.int32, (edge_rows, 1), 0)
    s.hid[PAD : PAD + edge_rows, :] = jnp.where(
        jnp.logical_or(has_low, at >= HALO), first_hidden(0, edge_rows), 0.0
    )
    s.hid[PAD + last : PAD + total, :] = jnp.where(
        jnp.logical_or(has_high, at < HALO), first_hidden(last, edge_rows), 0.0
    )
    conv_ends(s.hid, 2, s.w2)
    second_hidden(0, edge_rows)
    second_hidden(last, edge_rows)
    send_pool(0, HALO)
    send_pool(rows - HALO, HALO)
    own = s.pool[0]
    store = pltpu.make_async_copy(s.pool.at[0], s.emb_out, s.store_sem)
    store.start()

    for k in range(3):
        first = PAD + HALO + (k - 1) * 2
        s.hid_t[k * channels : (k + 1) * channels, :] = jnp.transpose(s.hid[first : first + rows, :].astype(BF16))
    s.hid2_t[...] = jnp.transpose(s.hid2[HALO : HALO + rows, :])

    col = lax.broadcasted_iota(jnp.int32, (rows, 1), 0)
    row = lax.broadcasted_iota(jnp.int32, (1, rows), 1)
    live = (col < own_count).astype(F32)
    first = z * rows
    offs_row = s.off[...]
    offs_col = jnp.transpose(jnp.broadcast_to(offs_row.astype(F32), (LANES, rows)))[:, 0:1].astype(jnp.int32)
    target_col = jnp.where(first + col - offs_col >= 0, col - offs_col, col + offs_col)
    target_row = jnp.where(first + row - offs_row >= 0, row - offs_row, row + offs_row)
    live_row = (row < own_count).astype(F32)
    band = jnp.where(target_col == row, live, 0.0) + jnp.where(target_row == col, live_row, 0.0)
    paired = jnp.dot(band.astype(BF16), own, preferred_element_type=F32)
    edge = lax.broadcasted_iota(jnp.int32, (1, HALO), 1)
    band_low = jnp.where(target_col == edge - HALO, live, 0.0)
    paired += jnp.dot(band_low.astype(BF16), s.emb_ext[0:HALO, :], preferred_element_type=F32)
    nextm.wait_recv()
    next_off = s.meta_next[0:1, 0:HALO]
    next_live = jnp.where(jnp.logical_and(has_high, edge < s.meta_next[1:2, 0:HALO]), 1.0, 0.0)
    band_high = jnp.where(rows + edge - next_off == col, next_live, 0.0)
    paired += jnp.dot(band_high.astype(BF16), s.emb_ext[HALO + rows :, :], preferred_element_type=F32)

    for copy in mpools:
        copy.wait_recv()

    def count_of(m):
        return own_count if m == 0 else s.meta_pool[m - 1, 1:2, 0:1]

    diag = col == row

    def scored(a_block, m):
        score = lax.dot_general(a_block, s.pool[m], (((1,), (1,)), ((), ())), preferred_element_type=F32)
        return jnp.exp(2.0 * score - 2.0)

    def summed(x, m):
        return jnp.sum(jnp.where(row < count_of(m), x, 0.0), axis=1, keepdims=True)

    x0 = jnp.where(diag, 0.0, scored(own, 0))
    s.xs[0] = x0.astype(BF16)
    denom = summed(x0, 0)
    for copies in pools:
        for copy in copies:
            copy.wait_recv()
    crossed = []
    for m in range(1, n_batch):
        x = scored(own, m)
        s.xs[m] = x.astype(BF16)
        denom += summed(x, m)
        crossed.append(x)

    def set_rhs(a, a_live, a_denom):
        value = s.pool[a].astype(F32) * a_live
        s.rhs[a, :, 0:LANES] = value.astype(BF16)
        s.rhs[a, :, LANES : 2 * LANES] = (value / a_denom).astype(BF16)

    set_rhs(0, live, denom)
    if n_batch == 2:
        across = jnp.sum(jnp.where(col < own_count, crossed[0], 0.0), axis=0, keepdims=True)
        other_denom = jnp.transpose(jnp.broadcast_to(across, (LANES, rows)))[:, 0:1]
        other_denom += summed(jnp.where(diag, 0.0, scored(s.pool[1], 1)), 1)
        set_rhs(1, (col < count_of(1)).astype(F32), other_denom)
    else:
        def one(a, carry):
            value = s.pool[a]
            den = jnp.zeros((rows, 1), F32)
            for m in range(n_batch):
                den += summed(jnp.where(jnp.logical_and(diag, a == m), 0.0, scored(value, m)), m)
            a_count = s.meta_pool[a - 1][1:2, 0:1]
            set_rhs(a, (col < a_count).astype(F32), den)
            return carry

        lax.fori_loop(1, n_batch, one, 0)
    acc = jnp.dot(s.xs[0], s.rhs[0], preferred_element_type=F32)
    for m in range(1, n_batch):
        acc += jnp.dot(s.xs[m], s.rhs[m], preferred_element_type=F32)
    unit = s.unit[HALO : HALO + rows, :]
    scale = s.scale[HALO : HALO + rows, :]
    grad_unit = 2.0 * (live * (acc[:, 0:LANES] / denom + acc[:, LANES:]) - paired)
    along = jnp.sum(unit * grad_unit, axis=1, keepdims=True)
    gf = ((grad_unit - unit * along) * scale).astype(BF16)
    gh = lax.dot_general(gf, s.proj[...], (((1,), (1,)), ((), ())), preferred_element_type=F32)
    gp = (gh * s.slope[HALO : HALO + rows, :]).astype(BF16)
    s.gp[...] = gp

    def with_bias(value):
        top = value[..., 0:body, :].astype(BF16)
        bias = value[..., body : body + PAD, :] + value[..., body + PAD :, :]
        high = bias.astype(BF16)
        return top, high, (bias - high.astype(F32)).astype(BF16)

    def put_p(ref, value):
        top, high, rest = with_bias(value)
        ref[..., 0:body, :] = top
        ref[..., body:, :] = jnp.concatenate([high, rest], axis=-2)

    reps, bats, tms, gats = {}, {}, {}, {}

    def produce(c):
        value = jnp.dot(s.hid_t[c * span : (c + 1) * span, :], s.gp[...], preferred_element_type=F32)
        for owner in range(2):
            for i in range(n_tm):
                s.grads[c, owner, i, :, 0:share] = value[
                    owner * half : (owner + 1) * half, i * share : (i + 1) * share
                ].astype(BF16)
        reps[c] = send(s.grads.at[c, other], s.rep_in.at[c], s.rep_sem, (c,), {"rep": other})

    def over_batch(c):
        reps[c].wait_recv()
        s.part_one[c] = (s.grads[c, r].astype(F32) + s.rep_in[c].astype(F32)).astype(BF16)
        bats[c] = [
            send(
                s.part_one.at[c, :, pl.ds(pl.multiple_of(lax.rem(b + o, n_batch) * piece, piece), piece)],
                s.batch_in.at[c, o - 1], s.batch_sem, (c, o - 1), batch_at(o),
            )
            for o in range(1, n_batch)
        ]

    def over_tm(c):
        value = s.part_one[c, :, pl.ds(pl.multiple_of(b * piece, piece), piece)].astype(F32)
        for o in range(1, n_batch):
            bats[c][o - 1].wait_recv()
            value += s.batch_in[c, o - 1].astype(F32)
        s.part_two[c] = value.astype(BF16)
        tms[c] = [
            send(s.part_two.at[c, lax.rem(z + o, n_tm)], s.tm_in.at[c, o - 1], s.tm_sem, (c, o - 1), tm_at(o))
            for o in range(1, n_tm)
        ]

    def finish(c):
        value = s.part_two[c, z].astype(F32)
        for o in range(1, n_tm):
            tms[c][o - 1].wait_recv()
            value += s.tm_in[c, o - 1].astype(F32)
        at = pl.ds(pl.multiple_of(c * span + r * half + b * piece, piece), piece)
        s.final[at, :] = value.astype(BF16)
        mine = s.final.at[at]
        if c in early:
            gats[c] = [send(mine, mine, s.gat_sem, (c, 2 * o - 1), batch_at(o)) for o in range(1, n_batch)]
            return
        gats[c] = [send(mine, mine, s.gat_sem, (c, 0), {"rep": other})]
        for o in range(1, n_batch):
            gats[c].append(send(mine, mine, s.gat_sem, (c, 2 * o - 1), batch_at(o)))
            gats[c].append(send(mine, mine, s.gat_sem, (c, 2 * o), across_at(o)))

    p_copies = {}

    def make_p():
        ones = jnp.ones((HALO, rows), BF16)
        bias = jnp.dot(ones, s.gp[...], preferred_element_type=F32)
        proj = jnp.dot(s.hid2_t[...], gf, preferred_element_type=F32)
        high = bias.astype(BF16)
        rest = (bias - high.astype(F32)).astype(BF16)
        bias = jnp.concatenate([high[0:PAD], rest[0:PAD]], axis=0)
        for i in range(n_tm):
            for owner in range(2):
                begin = i * share + owner * body
                s.p_grads[owner, i, 0:body, :] = proj[begin : begin + body, :].astype(BF16)
                s.p_grads[owner, i, body:, 0:share] = bias[:, i * share : (i + 1) * share]
        p_copies["rep"] = send(s.p_grads.at[other], s.p_rep, s.p_sem, (0,), {"rep": other})

    def p_over_tm():
        p_copies["rep"].wait_recv()
        put_p(s.p_one, s.p_grads[r].astype(F32) + s.p_rep[...].astype(F32))
        p_copies["tm"] = [
            send(s.p_one.at[lax.rem(z + o, n_tm)], s.p_tm.at[o - 1], s.p_tm_sem, (o - 1,), tm_at(o))
            for o in range(1, n_tm)
        ]

    def p_over_batch():
        value = s.p_one[z].astype(F32)
        for o in range(1, n_tm):
            p_copies["tm"][o - 1].wait_recv()
            value += s.p_tm[o - 1].astype(F32)
        put_p(s.p_part.at[b], value)
        p_copies["batch"] = [
            send(s.p_part.at[b], s.p_part.at[b], s.p_batch_sem, (o - 1,), batch_at(o)) for o in range(1, n_batch)
        ]

    def p_finish():
        for copy in p_copies["batch"]:
            copy.wait_recv()
        value = s.p_part[0].astype(F32)
        for i in range(1, n_batch):
            value += s.p_part[i].astype(F32)
        at = pl.ds(pl.multiple_of(3 * channels + r * extra, HALO), extra)
        put_p(s.final.at[at], value)
        mine = s.final.at[at]
        gats[chunks] = [send(mine, mine, s.p_gat_sem, (), {"rep": other})]

    def tm_first(c):
        reps[c].wait_recv()
        s.part_one[c] = (s.grads[c, r].astype(F32) + s.rep_in[c].astype(F32)).astype(BF16)
        tms[c] = [
            send(s.part_one.at[c, lax.rem(z + o, n_tm)], s.zf_tm.at[c, o - 1], s.tm_sem, (c, o - 1), tm_at(o))
            for o in range(1, n_tm)
        ]

    def then_batch(c):
        value = s.part_one[c, z].astype(F32)
        for o in range(1, n_tm):
            tms[c][o - 1].wait_recv()
            value += s.zf_tm[c, o - 1].astype(F32)
        s.zf_part[c, b] = value.astype(BF16)
        mine = s.zf_part.at[c, b]
        bats[c] = [send(mine, mine, s.batch_sem, (c, o - 1), batch_at(o)) for o in range(1, n_batch)]

    def finish_tm_first(c):
        for copy in bats[c]:
            copy.wait_recv()
        value = s.zf_part[c, 0].astype(F32)
        for i in range(1, n_batch):
            value += s.zf_part[c, i].astype(F32)
        at = pl.ds(pl.multiple_of(c * span + r * half, half), half)
        s.final[at, :] = value.astype(BF16)
        mine = s.final.at[at]
        gats[c] = [send(mine, mine, s.gat_sem, (c, 0), {"rep": other})]

    ring = list(range(TM_FIRST))
    early = range(TM_FIRST, chunks - 2)
    line = list(range(TM_FIRST, chunks))
    produce(line[0])
    for c in ring:
        produce(c)
    if not ring:
        produce(line[1])
    over_batch(line[0])
    for c in ring:
        tm_first(c)
    if ring:
        produce(line[1])
    make_p()
    over_batch(line[1])
    produce(line[2])
    p_over_tm()
    for i in range(3, len(line)):
        produce(line[i])
        over_batch(line[i - 1])
    over_batch(line[-1])
    for step in range(len(line) + LAG):
        if step < len(line):
            over_tm(line[step])
        if step == 2:
            for c in ring:
                then_batch(c)
            p_over_batch()
        if step == len(line) - 1:
            for c in ring:
                finish_tm_first(c)
            p_finish()
        if step >= LAG:
            finish(line[step - LAG])
    for c in early:
        for copy in gats[c]:
            copy.wait_recv()
        mine = s.final.at[pl.ds(pl.multiple_of(c * span + r * half, half), half)]
        gats[c] = [send(mine, mine, s.gat_sem, (c, 0), {"rep": other})]
    stores = [store]
    for c in [*ring, chunks, *line]:
        for copy in gats[c]:
            copy.wait_recv()
        at = pl.ds(c * span, span) if c < chunks else pl.ds(3 * channels, 2 * extra)
        stores.append(pltpu.make_async_copy(s.final.at[at], s.sums_out.at[at], s.sums_sem.at[c]))
        stores[-1].start()
    for copy in stores:
        copy.wait()
    for copy in started:
        copy.wait_send()


def spread(share, emb_ref, sums_ref, emb_out, conv_out, bias_out, proj_out, emb, sums, conv, bias, proj, sem):
    channels = conv.shape[1]
    rest = 3 * channels
    body = share // 2
    keep = pltpu.make_async_copy(emb_ref, emb, sem.at[0])
    keep.start()
    parts = [(rest, sums.shape[0] - rest)] + [(k * channels, channels) for k in range(3)]
    loads = []
    for i, (begin, count) in enumerate(parts):
        at = pl.ds(begin, count)
        loads.append(pltpu.make_async_copy(sums_ref.at[at], sums.at[at], sem.at[1 + i]))
        loads[-1].start()
    stores = []

    def store(src, dst):
        stores.append(pltpu.make_async_copy(src, dst, sem.at[5 + len(stores)]))
        stores[-1].start()

    loads[0].wait()
    for owner in range(2):
        begin = rest + owner * (body + HALO)
        proj[owner * body : (owner + 1) * body, :] = sums[begin : begin + body, :].astype(F32)
    value = sums[rest + body : rest + body + HALO, :].astype(F32)
    bias[...] = (value[0:PAD] + value[PAD:])[0:1, 0:share]
    store(proj, proj_out)
    store(bias, bias_out)
    keep.wait()
    store(emb, emb_out)
    for k in range(3):
        loads[1 + k].wait()
        conv[k] = sums[k * channels : (k + 1) * channels, :].astype(F32)[:, 0:share]
        store(conv.at[k], conv_out.at[k])
    for copy in stores:
        copy.wait()


def per_device(
    n_tm, n_batch,
    latents, session_ids, session_gain, session_shift, first_conv_weight, first_conv_bias,
    second_conv_weight, second_conv_bias, proj_weight, offsets, counts,
):
    rows, channels = latents.shape[1:]
    emb = proj_weight.shape[1]
    sessions = session_gain.shape[0]
    total = rows + 2 * HALO
    share = channels // n_tm
    span = channels // HALVES
    half = span // 2
    piece = half // n_batch
    chunks = 3 * HALVES
    extra = share // 2 + HALO
    out_rows = 3 * channels + 2 * extra
    hbm = pl.BlockSpec(memory_space=pl.ANY)
    nb = n_batch - 1
    dma = pltpu.SemaphoreType.DMA
    inputs = ("lat", "sid", "cnt", "gain", "shift", "w1", "b1", "w2", "b2", "proj", "off")
    outputs = ("emb_out", "sums_out")
    scratch = {
        "lat": pltpu.VMEM((rows, channels), BF16),
        "sid": pltpu.SMEM((1,), jnp.int32),
        "cnt": pltpu.SMEM((1, 1), jnp.int32),
        "gain": pltpu.VMEM((sessions, channels), F32),
        "shift": pltpu.VMEM((sessions, channels), F32),
        "w1": pltpu.VMEM((3 * channels, channels), BF16),
        "b1": pltpu.VMEM((1, channels), F32),
        "w2": pltpu.VMEM((3 * channels, channels), BF16),
        "b2": pltpu.VMEM((1, channels), F32),
        "proj": pltpu.VMEM((channels, emb), BF16),
        "off": pltpu.VMEM((1, rows), jnp.int32),
        "halo": pltpu.VMEM((2, HALO, channels), BF16),
        "meta": pltpu.VMEM((8, LANES), jnp.int32),
        "meta_next": pltpu.VMEM((8, LANES), jnp.int32),
        "meta_pool": pltpu.VMEM((nb, 8, LANES), jnp.int32),
        "ext": pltpu.VMEM((total + 2 * PAD, channels), F32),
        "hid": pltpu.VMEM((total + 2 * PAD, channels), F32),
        "taps": pltpu.VMEM((total, 3 * channels), BF16),
        "pre": pltpu.VMEM((total, channels), F32),
        "slope": pltpu.VMEM((total, channels), F32),
        "hid2": pltpu.VMEM((total, channels), BF16),
        "unit": pltpu.VMEM((total, emb), F32),
        "scale": pltpu.VMEM((total, LANES), F32),
        "emb_ext": pltpu.VMEM((total, emb), BF16),
        "pool": pltpu.VMEM((n_batch, rows, emb), BF16),
        "xs": pltpu.VMEM((n_batch, rows, rows), BF16),
        "rhs": pltpu.VMEM((n_batch, rows, 2 * emb), BF16),
        "hid_t": pltpu.VMEM((3 * channels, rows), BF16),
        "hid2_t": pltpu.VMEM((channels, rows), BF16),
        "gp": pltpu.VMEM((rows, channels), BF16),
        "p_grads": pltpu.VMEM((2, n_tm, extra, LANES), BF16),
        "p_rep": pltpu.VMEM((n_tm, extra, LANES), BF16),
        "p_one": pltpu.VMEM((n_tm, extra, LANES), BF16),
        "p_tm": pltpu.VMEM((n_tm - 1, extra, LANES), BF16),
        "p_part": pltpu.VMEM((n_batch, extra, LANES), BF16),
        "grads": pltpu.VMEM((chunks, 2, n_tm, half, LANES), BF16),
        "rep_in": pltpu.VMEM((chunks, n_tm, half, LANES), BF16),
        "part_one": pltpu.VMEM((chunks, n_tm, half, LANES), BF16),
        "batch_in": pltpu.VMEM((chunks, nb, n_tm, piece, LANES), BF16),
        "part_two": pltpu.VMEM((chunks, n_tm, piece, LANES), BF16),
        "tm_in": pltpu.VMEM((chunks, n_tm - 1, piece, LANES), BF16),
        "zf_tm": pltpu.VMEM((max(TM_FIRST, 1), n_tm - 1, half, LANES), BF16),
        "zf_part": pltpu.VMEM((max(TM_FIRST, 1), n_batch, half, LANES), BF16),
        "final": pltpu.VMEM((out_rows, LANES), BF16),
        "load_sem": dma((len(inputs),)),
        "store_sem": dma,
        "sums_sem": dma((chunks + 1,)),
        "halo_sem": dma((2, 2)),
        "meta_sem": dma((2, 1)),
        "mpool_sem": dma((2, nb)),
        "pool_sem": dma((2, INNER_BLOCKS + 2, nb)),
        "p_sem": dma((2, 1)),
        "p_tm_sem": dma((2, n_tm - 1)),
        "p_batch_sem": dma((2, nb)),
        "p_gat_sem": dma((2,)),
        "rep_sem": dma((2, chunks)),
        "batch_sem": dma((2, chunks, nb)),
        "tm_sem": dma((2, chunks, n_tm - 1)),
        "gat_sem": dma((2, chunks, 2 * nb + 1)),
    }
    names = tuple(n + "_hbm" for n in inputs) + outputs + tuple(scratch)
    embed, sums = pl.pallas_call(
        functools.partial(kernel, n_tm, n_batch, names),
        out_shape=(
            jax.ShapeDtypeStruct((rows, emb), BF16),
            jax.ShapeDtypeStruct((out_rows, LANES), BF16),
        ),
        in_specs=[hbm] * len(inputs),
        out_specs=(hbm, hbm),
        scratch_shapes=list(scratch.values()),
        compiler_params=pltpu.CompilerParams(
            collective_id=0, has_side_effects=True, vmem_limit_bytes=56 * 1024 * 1024
        ),
    )(
        latents[0], session_ids, counts, session_gain, session_shift,
        first_conv_weight.reshape(3 * channels, channels), first_conv_bias[None],
        second_conv_weight.reshape(3 * channels, channels), second_conv_bias[None],
        proj_weight, offsets,
    )
    embed, conv, bias, proj = pl.pallas_call(
        functools.partial(spread, share),
        out_shape=(
            jax.ShapeDtypeStruct((rows, emb), BF16),
            jax.ShapeDtypeStruct((3, channels, share), F32),
            jax.ShapeDtypeStruct((1, share), F32),
            jax.ShapeDtypeStruct((share, emb), F32),
        ),
        in_specs=[hbm, hbm],
        out_specs=(hbm, hbm, hbm, hbm),
        scratch_shapes=[
            pltpu.VMEM((rows, emb), BF16),
            pltpu.VMEM((out_rows, LANES), BF16),
            pltpu.VMEM((3, channels, share), F32),
            pltpu.VMEM((1, share), F32),
            pltpu.VMEM((share, emb), F32),
            dma((11,)),
        ],
    )(embed, sums)
    return embed[None], conv, bias[0], proj


def solution(mesh):
    return jax.shard_map(
        functools.partial(per_device, mesh.shape["tm"], mesh.shape["batch"]),
        mesh=mesh,
        in_specs=(
            P(("groups", "batch", "rep"), "tm", None),
            P(("groups", "batch", "rep")),
            P(),
            P(),
            P(),
            P(),
            P(),
            P(),
            P(),
            P(("groups", "batch", "rep"), "tm"),
            P(("groups", "batch", "rep"), "tm"),
        ),
        out_specs=(
            P(("groups", "batch", "rep"), "tm", None),
            P("groups", None, "tm"),
            P(("groups", "tm")),
            P(("groups", "tm"), None),
        ),
        check_vma=False,
    )
```
